32 devices in a mesh: ctx: 8 (over y, x, core), fsdp: 4 (over z).
Axes of the slice: x: 2, y: 2, z: 4, core: 2. Of those that a mesh axis runs over, the one named last changes fastest.
Arguments:
- tokens: bfloat16 [10240, 768], P(('ctx', 'fsdp')), may hold values from -6 to 6
- lengths: int32 [4, 3], P('fsdp'), may hold values from 1 to 1280, 2560 in all within a row
- deal_table: int32 [4, 8, 8], P('fsdp'), may hold values from 0 to 7, each once within a row
- norm_one_gain: bfloat16 [768], P('fsdp'), may hold values from 0.099609375 to 1.8984375
- norm_one_bias: bfloat16 [768], P('fsdp'), may hold values from -3 to 3
- triple_weight: bfloat16 [768, 2304], P('fsdp'), may hold values from -1 to 1
- output_weight: bfloat16 [768, 768], P('fsdp'), may hold values from -0.4375 to 0.4375
- norm_two_gain: bfloat16 [768], P('fsdp'), may hold values from 0.099609375 to 1.8984375
- norm_two_bias: bfloat16 [768], P('fsdp'), may hold values from -3 to 3
- up_weight: bfloat16 [768, 3072], P('fsdp'), may hold values from -0.21875 to 0.21875
- down_weight: bfloat16 [3072, 768], P('fsdp'), may hold values from -0.15625 to 0.15625
- cotangent: bfloat16 [10240, 768], P(('ctx', 'fsdp')), may hold values from -6 to 6
Outputs:
- result: bfloat16 [10240, 768], P(('ctx', 'fsdp'))
- token_grad: float32 [10240, 768], P(('ctx', 'fsdp'))
- norm_one_gain_grad: float32 [768], P('fsdp')
- norm_one_bias_grad: float32 [768], P('fsdp')
- triple_weight_grad: float32 [768, 2304], P('fsdp')
- output_weight_grad: float32 [768, 768], P('fsdp')
- norm_two_gain_grad: float32 [768], P('fsdp')
- norm_two_bias_grad: float32 [768], P('fsdp')
- up_weight_grad: float32 [768, 3072], P('fsdp')
- down_weight_grad: float32 [3072, 768], P('fsdp')
The draws below stay inside these ranges and needn't reach their ends.
Inputs may be any that keep to these rules, and one draw needn't show every extreme that they name: Row f gives the lengths of the 3 sequences packed in order into group f's 2560 positions; they sum to 2560, and the longest is exactly 1280. For every group f and natural block s, deal_table[f, s] is a permutation of 0 .. 7.
All inputs are finite; a program needn't handle non-finite values.
Results may differ from the reference program's by a relative error of at most 0.025.
The reference program's roundings to bfloat16 on the way count: a program that leaves them out, or rounds other values in their place, can miss the bound.
Values may be sent and summed in bfloat16 or wider, within the bound.
No kernel may reach another device: no remote copies, remote signals or barrier semaphores. Data moves between devices by JAX's collectives and lax.ppermute only.
A program may use at most 256 MiB of HBM per device.

```python
import math
import jax
import jax.numpy as jnp
import numpy as np
from jax import lax

D = 768
HEADS = 12
HEAD = 64
FF = 3072
TOK_DEV = 320
PART = 40
GROUP = 2560
TOKENS = 10240
NSEQ = 3
LONGEST = 1280
N_CTX = 8
N_FSDP = 4


def draw_triple_weight(key, part):
    raw = jax.random.truncated_normal(key, -5.0, 5.0, (D, 3 * D), jnp.float32) / math.sqrt(D)
    column = jnp.arange(3 * D)
    factor = jnp.where(column < HEAD, 6.0 / LONGEST, 1.0)
    return (raw * factor).astype(jnp.bfloat16)


def block_levels(own_key, extent, cuts, low, largest):
    def one(axis_at, shards_of):
        heights = jax.random.uniform(jax.random.fold_in(jax.random.fold_in(own_key, 6), axis_at), (shards_of,), jnp.float32, low / len(cuts), largest / len(cuts))
        return jnp.repeat(jnp.exp(heights), extent[axis_at] // shards_of).reshape((-1,) + (1,) * (len(extent) - axis_at - 1))

    gain = one(*cuts[0])
    for cut in cuts[1:]:
        gain = gain * one(*cut)
    return gain


def split_up(count, total, reach, slope):
    loads = [(1 << 20) // math.isqrt(rank ** slope) + 1 for rank in range(2, count + 1)]
    rest, holding = total - reach - (count - 1), [1] * (count - 1)
    while rest > 0:
        candidates = [i for i in range(count - 1) if holding[i] < reach]
        mass, budget = sum([loads[i] for i in candidates]), rest
        for i in candidates:
            addition = min(reach - holding[i], max(1, budget * loads[i] // mass), rest)
            holding[i] = holding[i] + addition
            rest = rest - addition
    return np.array([reach] + holding)


def ragged(key, amount, total, bound, skew):
    if amount == 2:
        one = jax.random.randint(key, (), max(1, total - bound), min(bound, total - 1) + 1)
        return jnp.stack([one, total - one])
    tallies = jnp.asarray(split_up(amount, total, bound, skew), jnp.int32)
    couples = (amount - 1) // 2
    donor, taker = tallies[1:1 + 2 * couples:2], tallies[2:2 + 2 * couples:2]
    room = jnp.minimum(donor - 1, bound - taker)
    passed = jax.random.randint(jax.random.fold_in(key, 1), (couples,), 0, 1 << 20) % (room + 1)
    tallies = tallies.at[1:1 + 2 * couples:2].set(donor - passed).at[2:2 + 2 * couples:2].set(taker + passed)
    return tallies[jax.random.permutation(jax.random.fold_in(key, 2), amount)]


def noise(key, shape, deviation, most, split=(), kind=jnp.bfloat16):
    drawn = jax.random.normal(key, shape, jnp.float32) * deviation
    if len(split) > 0:
        drawn = block_levels(key, shape, split, -0.22, 0.18) * drawn
    return jnp.clip(drawn, min=-most, max=most).astype(kind)


def setup_inputs(seed: int = 0) -> dict:
    key_of = jax.random.split(jax.random.key(seed), 13)
    tokens = noise(key_of[0], (TOKENS, D), 1.0, 6.0, ((0, 32),))
    lengths = jax.vmap(lambda own: ragged(own, NSEQ, GROUP, LONGEST, 2))(jax.random.split(key_of[1], N_FSDP)).reshape((N_FSDP, NSEQ)).astype(jnp.int32)
    deal_table = jax.vmap(lambda own: jax.random.permutation(own, N_CTX))(jax.random.split(key_of[2], N_FSDP * N_CTX)).reshape((N_FSDP, N_CTX, N_CTX)).astype(jnp.int32)
    norm_one_gain = jnp.clip(1.0 + 0.18 * jax.random.normal(key_of[3], (D,), jnp.float32), 0.099609375, 1.8984375).astype(jnp.bfloat16)
    norm_one_bias = noise(key_of[4], (D,), 0.3, 3.0, ((0, 4),))
    triple_weight = draw_triple_weight(jax.random.fold_in(key_of[12], 71), 0)
    output_weight = noise(key_of[6], (D, D), (D // 4) ** -0.5, 0.4375, ((0, 4),))
    norm_two_gain = jnp.clip(1.0 + 0.18 * jax.random.normal(key_of[7], (D,), jnp.float32), 0.099609375, 1.8984375).astype(jnp.bfloat16)
    norm_two_bias = noise(key_of[8], (D,), 0.3, 3.0, ((0, 4),))
    up_weight = noise(key_of[9], (D, FF), D ** -0.5, 0.21875, ((0, 4),))
    down_weight = noise(key_of[10], (FF, D), (FF // 2) ** -0.5, 0.15625, ((0, 4),))
    cotangent = noise(key_of[11], (TOKENS, D), 1.0, 6.0, ((0, 32),))
    return {"tokens": tokens, "lengths": lengths, "deal_table": deal_table, "norm_one_gain": norm_one_gain, "norm_one_bias": norm_one_bias, "triple_weight": triple_weight, "output_weight": output_weight, "norm_two_gain": norm_two_gain, "norm_two_bias": norm_two_bias, "up_weight": up_weight, "down_weight": down_weight, "cotangent": cotangent}


@jax.custom_vjp
def low(v):
    return lax.optimization_barrier(v.astype(jnp.bfloat16)).astype(jnp.float32)

@jax.custom_vjp
def low_back(v):
    return v

def low_keep(v):
    return (low(v), None)

def low_pass(kept, grad):
    return (grad,)

def back_keep(v):
    return (v, None)

def back_low(kept, grad):
    return (low(grad),)
low.defvjp(low_keep, low_pass)
low_back.defvjp(back_keep, back_low)
EPS = 1e-05
HIGH = lax.Precision.HIGHEST

def layer_norm(values, gain_vec, offset):
    center = values - lax.optimization_barrier(jnp.mean(values, axis=-1, keepdims=True))
    spread = lax.optimization_barrier(jnp.mean(center * center, axis=-1, keepdims=True))
    return center * lax.rsqrt(spread + EPS) * gain_vec + offset

def product(left_side, right_side):
    return jnp.dot(left_side, right_side, precision=HIGH, preferred_element_type=jnp.float32)

def block_math(carry_sum, query_block, seg_query, pos_query, key_heads, value_heads, seg_key, first_key):
    head_scale = 1.0 / math.sqrt(HEAD)
    pos_key = jnp.arange(GROUP, dtype=jnp.int32)
    logits = low_back(jnp.einsum('qhe,khe->hqk', query_block, key_heads, precision=HIGH, preferred_element_type=jnp.float32) * head_scale)
    same_seq = seg_query[:, None] == seg_key[None, :]
    allowed = same_seq & (pos_key[None, :] <= pos_query[:, None])
    chosen = same_seq & (pos_key[None, :] < pos_query[:, None]) & jnp.logical_not(first_key)[None, :]
    select = jnp.where(chosen, jax.nn.relu(logits[0]), 0.0)
    prior_sum = carry_sum[None, :] + jnp.cumsum(select, axis=0) - select
    expo_block = jnp.where(allowed[None], jnp.exp(logits - prior_sum[None]), 0.0)
    total_sum = lax.optimization_barrier(jnp.sum(expo_block, axis=-1))
    numer_sum = low_back(jnp.einsum('hqk,khe->qhe', low(expo_block), value_heads, precision=HIGH, preferred_element_type=jnp.float32))
    attn_mixed = numer_sum / total_sum.T[:, :, None]
    return (carry_sum + lax.optimization_barrier(jnp.sum(select, axis=0)), attn_mixed.reshape(query_block.shape[0], D))

def group_attention(inputs):
    query_group, key_group, value_group, seq_lens = inputs
    block_rows = math.gcd(GROUP, 512)
    block_count = GROUP // block_rows
    positions = jnp.arange(GROUP, dtype=jnp.int32)
    seq_ends = jnp.cumsum(seq_lens).astype(jnp.int32)
    seq_starts = (seq_ends - seq_lens).astype(jnp.int32)
    segment = lax.optimization_barrier(jnp.sum((positions[:, None] >= seq_ends[None, :]).astype(jnp.int32), axis=1))
    first_key = jnp.any(positions[:, None] == seq_starts[None, :], axis=1)
    key_heads = key_group.reshape(GROUP, HEADS, HEAD)
    value_heads = value_group.reshape(GROUP, HEADS, HEAD)
    query_blocks = query_group.reshape(block_count, block_rows, HEADS, HEAD)
    seg_blocks = segment.reshape(block_count, block_rows)
    pos_blocks = positions.reshape(block_count, block_rows)
    checked = jax.checkpoint(block_math)

    def scan_step(carry_sum, slices):
        return checked(carry_sum, slices[0], slices[1], slices[2], key_heads, value_heads, segment, first_key)
    unused, mixed_blocks = lax.scan(scan_step, jnp.zeros((GROUP,), jnp.float32), (query_blocks, seg_blocks, pos_blocks))
    return mixed_blocks.reshape(GROUP, D)

def grouped(array):
    return array.reshape(N_CTX, N_FSDP, TOK_DEV, D).transpose(1, 0, 2, 3).reshape(N_FSDP, GROUP, D)

def ungrouped(array):
    return array.reshape(N_FSDP, N_CTX, TOK_DEV, D).transpose(1, 0, 2, 3).reshape(TOKENS, D)

def layer(x_all, weights, seq_lengths, deal_index):
    gain_one, bias_one, triple, output_w, gain_two, bias_two, up_w, down_w = weights
    hidden_one = low(layer_norm(x_all, gain_one, bias_one))
    projected = low_back(low(product(hidden_one, triple)))
    mixed = lax.map(group_attention, (grouped(projected[:, :D]), grouped(projected[:, D:2 * D]), grouped(projected[:, 2 * D:]), seq_lengths))
    mixed_low = low(ungrouped(mixed))
    attended = low_back(product(mixed_low, output_w))
    middle = x_all + attended
    hidden_two = low(layer_norm(middle, gain_two, bias_two))
    raised = low_back(product(hidden_two, up_w))
    activated = low(jax.nn.gelu(raised))
    lowered = low_back(product(activated, down_w))
    final = middle + lowered
    dealt = jax.vmap(lambda rows_of, row_order: jnp.take(rows_of, row_order, axis=0))(grouped(final), deal_index)
    return ungrouped(dealt)

def reference(tokens, lengths, deal_table, norm_one_gain, norm_one_bias, triple_weight, output_weight, norm_two_gain, norm_two_bias, up_weight, down_weight, cotangent):
    counter = jnp.arange(N_CTX, dtype=jnp.int32)
    route_hits = deal_table[:, :, :, None] == counter[None, None, None, :]
    inverse = lax.optimization_barrier(jnp.sum(jnp.where(route_hits, counter[None, None, :, None], 0), axis=2)).astype(jnp.int32)
    part_starts = (counter[None, :, None] * TOK_DEV + inverse * PART).astype(jnp.int32)
    deal_index = (jnp.transpose(part_starts, (0, 2, 1))[..., None] + jnp.arange(PART, dtype=jnp.int32)).reshape(N_FSDP, GROUP).astype(jnp.int32)
    weights = tuple([weight_arg.astype(jnp.float32) for weight_arg in (norm_one_gain, norm_one_bias, triple_weight, output_weight, norm_two_gain, norm_two_bias, up_weight, down_weight)])
    outcome, pullback = jax.vjp(lambda x_all, weight_set: layer(x_all, weight_set, lengths, deal_index), tokens.astype(jnp.float32), weights)
    grad_tokens, grads = pullback(cotangent.astype(jnp.float32))
    return (outcome.astype(jnp.bfloat16), grad_tokens, grads[0], grads[1], grads[2], grads[3], grads[4], grads[5], grads[6], grads[7])
```

```python
import functools
import math

import jax
import jax.numpy as jnp
from jax import lax
from jax.experimental import pallas as pl
from jax.experimental.pallas import tpu as pltpu
from jax.sharding import PartitionSpec as P

HEADS = 12
HEAD = 64
EPS = 1e-05
FAR = 1e30
SIDE = 128
VMEM_LIMIT = 60 * 1024 * 1024


def layer_norm(values, gain_vec, offset):
    center = values - jnp.mean(values, axis=-1, keepdims=True)
    spread = jnp.mean(center * center, axis=-1, keepdims=True)
    return center * lax.rsqrt(spread + EPS) * gain_vec + offset


def norm_back(values, gain_vec, grad_vec):
    center = values - jnp.mean(values, axis=-1, keepdims=True)
    spread = jnp.mean(center * center, axis=-1, keepdims=True)
    inv = lax.rsqrt(spread + EPS)
    unit = center * inv
    scaled = grad_vec * gain_vec
    mean_a = jnp.mean(scaled, axis=-1, keepdims=True)
    mean_b = jnp.mean(scaled * unit, axis=-1, keepdims=True)
    grad_in = inv * (scaled - mean_a - unit * mean_b)
    return grad_in, jnp.sum(grad_vec * unit, axis=0), jnp.sum(grad_vec, axis=0)


def gelu_back(values, grad_vec):
    unused, pullback = jax.vjp(jax.nn.gelu, values)
    return pullback(grad_vec)[0]


def matmul(left_side, right_side):
    return jnp.dot(left_side, right_side, preferred_element_type=jnp.float32)


def dot_tn(left_side, right_side):
    return lax.dot_general(
        left_side, right_side, (((0,), (0,)), ((), ())), preferred_element_type=jnp.float32
    )


def dot_nt(left_side, right_side):
    return lax.dot_general(
        left_side, right_side, (((1,), (1,)), ((), ())), preferred_element_type=jnp.float32
    )


class Plan:
    def __init__(self, row_count, n_ctx, n_seq, width):
        self.rows = row_count
        self.blocks = n_ctx
        self.part = row_count // n_ctx
        self.keys = row_count * n_ctx
        self.seqs = n_seq
        self.width = width
        self.small = self.keys <= 4096
        self.heads = 6 if self.small else 2
        self.groups = HEADS // self.heads
        self.step_groups = self.groups if self.small else 1
        self.steps = self.groups // self.step_groups
        self.span = self.heads * HEAD
        self.step_span = self.step_groups * self.span
        self.live = self.heads * self.part
        self.lanes = -(-(self.live + 1) // 128) * 128
        self.pairs = n_ctx * (n_ctx + 1) // 2
        self.part_pad = -(-self.part // 8) * 8


def scalar_start(plan, meta, position):
    start, end = 0, 0
    for n in range(plan.seqs):
        length = meta[n]
        end = end + length
        start = start + jnp.where(position >= end, length, 0)
    return start


def lane_parts(plan):
    lane = lax.broadcasted_iota(jnp.int32, (1, plan.lanes), 1)
    head = jnp.zeros_like(lane)
    for k in range(1, plan.heads):
        head = head + (lane >= k * plan.part).astype(jnp.int32)
    return lane, head, lane - head * plan.part


def block_copies(plan, step, t, kv, kb, vb, qk, sem):
    rows = pl.ds(pl.multiple_of(t * plan.rows, 8), plan.rows)
    k_at = pl.multiple_of(step * plan.step_span, 128)
    v_at = pl.multiple_of(plan.width + step * plan.step_span, 128)
    return (
        pltpu.make_async_copy(kv.at[rows, pl.ds(k_at, plan.step_span)], kb.at[t], sem.at[0, t]),
        pltpu.make_async_copy(kv.at[rows, pl.ds(v_at, plan.step_span)], vb.at[t], sem.at[1, t]),
        pltpu.make_async_copy(
            kv.at[rows, pl.ds(2 * plan.width, SIDE)], qk.at[t, :, pl.ds(0, SIDE)], sem.at[2, t]
        ),
        pltpu.make_async_copy(
            kv.at[rows, pl.ds(0, SIDE)], qk.at[t, :, pl.ds(SIDE, SIDE)], sem.at[3, t]
        ),
    )


def part_setup(plan, meta, s):
    lane, head, row = lane_parts(plan)
    offset = meta[plan.seqs + s] * plan.part
    first = s * plan.rows + offset
    pos = first + row
    start = scalar_start(plan, meta, pos)
    query = lax.broadcasted_iota(jnp.int32, (plan.rows, 1), 0)
    earlier = (query < offset + row) | (lane >= plan.live)
    block_pos = s * plan.rows + lax.broadcasted_iota(jnp.int32, (1, plan.rows), 1)
    return dict(
        lane=lane,
        pos=pos,
        start=start,
        earlier=earlier.astype(jnp.bfloat16),
        block_pos=block_pos,
        block_start=scalar_start(plan, meta, block_pos),
        select_from=scalar_start(plan, meta, s * plan.rows) // plan.rows,
        attend_from=scalar_start(plan, meta, first) // plan.rows,
    )


def masked_prior(plan, info, s, t, qk, acc):
    key = t * plan.rows + lax.broadcasted_iota(jnp.int32, (plan.rows, 1), 0)
    first = dot_nt(qk[t, :, SIDE : SIDE + HEAD], qk[s, :, :HEAD])
    chosen = (key < info["block_pos"]) & (key > info["block_start"])
    select = jnp.where(chosen, jnp.maximum(first, 0.0), 0.0)
    high = select.astype(jnp.bfloat16)
    rest = select - high.astype(jnp.float32)
    mid = rest.astype(jnp.bfloat16)
    low = (rest - mid.astype(jnp.float32)).astype(jnp.bfloat16)
    earlier = info["earlier"]
    sums = matmul(high, earlier) + matmul(mid, earlier) + matmul(low, earlier)
    before = acc[t]
    prior = before + sums
    acc[t] = before + jnp.broadcast_to(sums[:, plan.live : plan.live + 1], sums.shape)
    allowed = (key <= info["pos"]) & (key >= info["start"]) & (info["lane"] < plan.live)
    return jnp.where(allowed, prior, FAR)


def spread_rows(plan, rows_value, copies, own_head):
    return jnp.where(own_head, dot_tn(rows_value, copies), 0.0)


def head_masks(plan):
    lane, head, row = lane_parts(plan)
    live = lane < plan.live
    column_head = lax.broadcasted_iota(jnp.int32, (plan.span, 1), 0) // HEAD
    own_head = (column_head == head) & live
    copies = (lax.broadcasted_iota(jnp.int32, (plan.part, 1), 0) == row) & live
    return own_head, copies.astype(jnp.bfloat16)


def attend_kernel(
    plan, meta, q_ref, kv, high_ref, low_ref, total_ref, kb, vb, qk, vt, qbd, numer, total, acc, sem
):
    step = pl.program_id(0)

    def begin(t, carry):
        for copy in block_copies(plan, step, t, kv, kb, vb, qk, sem):
            copy.start()
        return carry

    lax.fori_loop(0, plan.blocks, begin, 0)
    own_head, copies = head_masks(plan)
    acc[...] = jnp.zeros_like(acc)

    def one_part(s, carry):
        for copy in block_copies(plan, step, s, kv, kb, vb, qk, sem):
            copy.wait()
        vt[s] = vb[s].T
        info = part_setup(plan, meta, s)
        q_part = q_ref[s]
        for g in range(plan.step_groups):
            cols = slice(g * plan.span, (g + 1) * plan.span)
            qbd[g] = spread_rows(plan, q_part[:, cols], copies, own_head).astype(jnp.bfloat16)
        numer[...] = jnp.zeros_like(numer)
        total[...] = jnp.zeros_like(total)

        def tile(t, carry):
            prior = masked_prior(plan, info, s, t, qk, acc)

            @pl.when(t >= info["attend_from"])
            def _():
                for g in range(plan.step_groups):
                    cols = slice(g * plan.span, (g + 1) * plan.span)
                    logits = matmul(kb[t, :, cols], qbd[g])
                    expo = jnp.exp(logits - prior)
                    total[g] += jnp.sum(expo.reshape(plan.rows // 8, 8, plan.lanes), axis=0)
                    numer[g] += matmul(vt[t, cols, :], expo.astype(jnp.bfloat16))

            return carry

        lax.fori_loop(info["select_from"], s + 1, tile, 0)
        for g in range(plan.step_groups):
            cols = slice(g * plan.span, (g + 1) * plan.span)
            whole = jnp.sum(total[g], axis=0, keepdims=True)
            whole = jnp.where(info["lane"] < plan.live, whole, 1.0)
            mixed = jnp.where(own_head, numer[g] / whole, 0.0)
            high = mixed.astype(jnp.bfloat16)
            low = (mixed - high.astype(jnp.float32)).astype(jnp.bfloat16)
            high_ref[s, :, cols] = dot_nt(copies, high).astype(jnp.bfloat16)
            low_ref[s, :, cols] = dot_nt(copies, low).astype(jnp.bfloat16)
            total_ref[0, g, pl.ds(s, 1), :] = whole
        return carry

    lax.fori_loop(0, plan.blocks, one_part, 0)


def attend(plan, meta, queries, kv):
    part_block = pl.BlockSpec((plan.blocks, plan.part, plan.step_span), lambda i, m: (0, 0, i))
    out = jax.ShapeDtypeStruct((plan.blocks, plan.part, plan.width), jnp.bfloat16)
    sg, nb = plan.step_groups, plan.blocks
    return pl.pallas_call(
        functools.partial(attend_kernel, plan),
        name="attend",
        grid_spec=pltpu.PrefetchScalarGridSpec(
            num_scalar_prefetch=1,
            grid=(plan.steps,),
            in_specs=[part_block, pl.BlockSpec(memory_space=pl.ANY)],
            out_specs=[
                part_block,
                part_block,
                pl.BlockSpec((1, sg, nb, plan.lanes), lambda i, m: (i, 0, 0, 0)),
            ],
            scratch_shapes=[
                pltpu.VMEM((nb, plan.rows, plan.step_span), jnp.bfloat16),
                pltpu.VMEM((nb, plan.rows, plan.step_span), jnp.bfloat16),
                pltpu.VMEM((nb, plan.rows, 2 * SIDE), jnp.bfloat16),
                pltpu.VMEM((nb, plan.step_span, plan.rows), jnp.bfloat16),
                pltpu.VMEM((sg, plan.span, plan.lanes), jnp.bfloat16),
                pltpu.VMEM((sg, plan.span, plan.lanes), jnp.float32),
                pltpu.VMEM((sg, 8, plan.lanes), jnp.float32),
                pltpu.VMEM((nb, plan.rows, plan.lanes), jnp.float32),
                pltpu.SemaphoreType.DMA((4, nb)),
            ],
        ),
        out_shape=[
            out,
            out,
            jax.ShapeDtypeStruct((plan.steps, sg, nb, plan.lanes), jnp.float32),
        ],
        compiler_params=pltpu.CompilerParams(vmem_limit_bytes=VMEM_LIMIT),
        cost_estimate=pl.CostEstimate(
            flops=4 * plan.rows * plan.keys * plan.width,
            bytes_accessed=4 * plan.keys * plan.width,
            transcendentals=plan.rows * plan.keys * HEADS,
        ),
    )(meta, queries.reshape(plan.blocks, plan.part, plan.width), kv)


def split_two(value):
    high = value.astype(jnp.bfloat16)
    return high, (value - high.astype(jnp.float32)).astype(jnp.bfloat16)


def back_kernel(
    plan,
    meta,
    q_ref,
    gm_ref,
    high_ref,
    low_ref,
    total_ref,
    kv,
    dq_ref,
    dk_ref,
    dv_ref,
    within_ref,
    sums_ref,
    kb,
    vb,
    qk,
    kt,
    qbd,
    sbd,
    ratio,
    dq,
    dk,
    dv,
    acc,
    stage,
    sem,
    out_sem,
):
    step = pl.program_id(0)

    def begin(t, carry):
        for copy in block_copies(plan, step, t, kv, kb, vb, qk, sem):
            copy.start()
        return carry

    lax.fori_loop(0, plan.blocks, begin, 0)
    own_head, copies = head_masks(plan)
    acc[...] = jnp.zeros_like(acc)
    dk[...] = jnp.zeros_like(dk)
    dv[...] = jnp.zeros_like(dv)

    @pl.when(step == 0)
    def _():
        sums_ref[...] = jnp.zeros_like(sums_ref)

    side_lane = lax.broadcasted_iota(jnp.int32, (1, SIDE), 1)

    def one_part(s, carry):
        for copy in block_copies(plan, step, s, kv, kb, vb, qk, sem):
            copy.wait()
        kt[s] = kb[s].T
        info = part_setup(plan, meta, s)
        q_part, gm_part = q_ref[s], gm_ref[s]
        high_part, low_part = high_ref[s], low_ref[s]
        for g in range(plan.step_groups):
            cols = slice(g * plan.span, (g + 1) * plan.span)
            whole = total_ref[0, g, pl.ds(s, 1), :]
            qbd[g] = spread_rows(plan, q_part[:, cols], copies, own_head).astype(jnp.bfloat16)
            gm_high, gm_low = split_two(gm_part[:, cols])
            grad = spread_rows(plan, gm_high, copies, own_head) + spread_rows(
                plan, gm_low, copies, own_head
            )
            mixed = spread_rows(plan, high_part[:, cols], copies, own_head) + spread_rows(
                plan, low_part[:, cols], copies, own_head
            )
            sbd[g] = (grad / whole).astype(jnp.bfloat16)
            ratio[g] = jnp.broadcast_to(
                jnp.sum(grad * mixed, axis=0, keepdims=True) / whole, (8, plan.lanes)
            )
        dq[...] = jnp.zeros_like(dq)
        lane_row = lax.broadcasted_iota(jnp.int32, (plan.lanes, 1), 0)
        row_at = lane_row
        for k in range(1, plan.heads):
            row_at = row_at - jnp.where(lane_row >= k * plan.part, plan.part, 0)
        fold = ((row_at > side_lane) & (side_lane < plan.part)) | (side_lane == plan.part + s)
        fold = jnp.where(fold & (lane_row < plan.live), -1.0, 0.0).astype(jnp.bfloat16)

        def tile(t, carry):
            prior = masked_prior(plan, info, s, t, qk, acc)

            @pl.when(t >= info["attend_from"])
            def _():
                within = jnp.zeros((plan.rows, SIDE), jnp.float32)
                for g in range(plan.step_groups):
                    cols = slice(g * plan.span, (g + 1) * plan.span)
                    logits = matmul(kb[t, :, cols], qbd[g])
                    expo = jnp.exp(logits - prior)
                    back = matmul(vb[t, :, cols], sbd[g])
                    gz = expo * (back - ratio[g, 0:1, :])
                    gz_high, gz_low = split_two(gz)
                    dv[t, :, cols] += dot_nt(expo.astype(jnp.bfloat16), sbd[g])
                    dk[t, :, cols] += dot_nt(gz_high, qbd[g])
                    dq[g] += matmul(kt[t, cols, :], gz_high)
                    within = within + matmul(gz_high, fold) + matmul(gz_low, fold)
                sums_ref[t] += jnp.where(side_lane < plan.part, 0.0, within)
                put_within(plan, within, s, t, within_ref, stage, out_sem)

            return carry

        lax.fori_loop(info["select_from"], s + 1, tile, 0)
        for g in range(plan.step_groups):
            cols = slice(g * plan.span, (g + 1) * plan.span)
            value = jnp.where(own_head, dq[g] * (1.0 / math.sqrt(HEAD)), 0.0)
            high, low = split_two(value)
            dq_ref[s, :, cols] = dot_nt(copies, high) + dot_nt(copies, low)
        return carry

    lax.fori_loop(0, plan.blocks, one_part, 0)

    def flush(t, carry):
        dk_ref[t] = dk[t].astype(jnp.bfloat16)
        dv_ref[t] = dv[t].astype(jnp.bfloat16)
        return carry

    lax.fori_loop(0, plan.blocks, flush, 0)


def pair_at(s, t):
    return s * (s + 1) // 2 + t


def put_within(plan, within, s, t, within_ref, stage, out_sem):
    if plan.small:
        within_ref[pair_at(s, t)] = within
        return
    stage[...] = within.T[: plan.part_pad, :]
    copy = pltpu.make_async_copy(stage, within_ref.at[pl.program_id(0), pair_at(s, t)], out_sem)
    copy.start()
    copy.wait()


def attend_back(plan, meta, queries, grad_mixed, high, low, total, kv):
    sg, nb = plan.step_groups, plan.blocks
    part_block = pl.BlockSpec((nb, plan.part, plan.step_span), lambda i, m: (0, 0, i))
    key_block = pl.BlockSpec((nb, plan.rows, plan.step_span), lambda i, m: (0, 0, i))
    pair_shape = (plan.pairs, plan.rows, SIDE)
    if plan.small:
        within_spec = pl.BlockSpec(pair_shape, lambda i, m: (0, 0, 0))
        within_shape = jax.ShapeDtypeStruct(pair_shape, jnp.float32)
    else:
        within_spec = pl.BlockSpec(memory_space=pl.ANY)
        pair_shape = (plan.steps, plan.pairs, plan.part_pad, plan.rows)
        within_shape = jax.ShapeDtypeStruct(pair_shape, jnp.float32)
    out = pl.pallas_call(
        functools.partial(back_kernel, plan),
        name="attend_back",
        grid_spec=pltpu.PrefetchScalarGridSpec(
            num_scalar_prefetch=1,
            grid=(plan.steps,),
            in_specs=[part_block] * 4
            + [
                pl.BlockSpec((1, sg, nb, plan.lanes), lambda i, m: (i, 0, 0, 0)),
                pl.BlockSpec(memory_space=pl.ANY),
            ],
            out_specs=[
                part_block,
                key_block,
                key_block,
                within_spec,
                pl.BlockSpec((nb, plan.rows, SIDE), lambda i, m: (0, 0, 0)),
            ],
            scratch_shapes=[
                pltpu.VMEM((nb, plan.rows, plan.step_span), jnp.bfloat16),
                pltpu.VMEM((nb, plan.rows, plan.step_span), jnp.bfloat16),
                pltpu.VMEM((nb, plan.rows, 2 * SIDE), jnp.bfloat16),
                pltpu.VMEM((nb, plan.step_span, plan.rows), jnp.bfloat16),
                pltpu.VMEM((sg, plan.span, plan.lanes), jnp.bfloat16),
                pltpu.VMEM((sg, plan.span, plan.lanes), jnp.bfloat16),
                pltpu.VMEM((sg, 8, plan.lanes), jnp.float32),
                pltpu.VMEM((sg, plan.span, plan.lanes), jnp.float32),
                pltpu.VMEM((nb, plan.rows, plan.step_span), jnp.float32),
                pltpu.VMEM((nb, plan.rows, plan.step_span), jnp.float32),
                pltpu.VMEM((nb, plan.rows, plan.lanes), jnp.float32),
                pltpu.VMEM((plan.part_pad, plan.rows), jnp.float32),
                pltpu.SemaphoreType.DMA((4, nb)),
                pltpu.SemaphoreType.DMA,
            ],
        ),
        out_shape=[
            jax.ShapeDtypeStruct((nb, plan.part, plan.width), jnp.float32),
            jax.ShapeDtypeStruct((nb, plan.rows, plan.width), jnp.bfloat16),
            jax.ShapeDtypeStruct((nb, plan.rows, plan.width), jnp.bfloat16),
            within_shape,
            jax.ShapeDtypeStruct((nb, plan.rows, SIDE), jnp.float32),
        ],
        compiler_params=pltpu.CompilerParams(vmem_limit_bytes=VMEM_LIMIT),
        cost_estimate=pl.CostEstimate(
            flops=10 * plan.rows * plan.keys * plan.width,
            bytes_accessed=12 * plan.keys * plan.width,
            transcendentals=plan.rows * plan.keys * HEADS,
        ),
    )(
        meta,
        queries.reshape(nb, plan.part, plan.width),
        grad_mixed.reshape(nb, plan.part, plan.width),
        high,
        low,
        total,
        kv,
    )
    return out


def first_kernel(plan, meta, q_ref, k_ref, later_ref, within_ref, dq_ref, dk_ref, stage, sem):
    dk_ref[...] = jnp.zeros_like(dk_ref)
    side_lane = lax.broadcasted_iota(jnp.int32, (1, SIDE), 1)
    row = lax.broadcasted_iota(jnp.int32, (1, plan.part), 1)

    def one_part(s, carry):
        first = s * plan.rows + meta[plan.seqs + s] * plan.part
        pos = first + row
        start = scalar_start(plan, meta, pos)
        attend_from = scalar_start(plan, meta, first) // plan.rows
        q_part = q_ref[s, :, :HEAD]

        def tile(t, total):
            k_tile = k_ref[pl.ds(pl.multiple_of(t * plan.rows, 8), plan.rows), :HEAD]
            key = t * plan.rows + lax.broadcasted_iota(jnp.int32, (plan.rows, 1), 0)
            logits = dot_nt(k_tile, q_part)
            chosen = (key < pos) & (key > start) & (logits > 0.0)
            if plan.small:
                within = within_ref[pair_at(s, t)]
            else:
                within = jnp.zeros((plan.part_pad, plan.rows), jnp.float32)
                for g in range(plan.steps):
                    copy = pltpu.make_async_copy(within_ref.at[g, pair_at(s, t)], stage, sem)
                    copy.start()
                    copy.wait()
                    within = within + stage[...]
                empty = jnp.zeros((SIDE - plan.part_pad, plan.rows), jnp.float32)
                within = jnp.concatenate([within, empty], axis=0).T
            later = jnp.sum(
                jnp.where(side_lane == s, later_ref[t], 0.0), axis=1, keepdims=True
            )
            extra = jnp.where(chosen, within[:, : plan.part] + later, 0.0).astype(jnp.bfloat16)
            dk_ref[t] += jnp.concatenate(
                [matmul(extra, q_part), jnp.zeros((plan.rows, SIDE - HEAD), jnp.float32)], axis=1
            )
            return total + dot_tn(extra, k_tile)

        total = lax.fori_loop(
            attend_from, s + 1, tile, jnp.zeros((plan.part, HEAD), jnp.float32)
        )
        dq_ref[s] = jnp.concatenate(
            [
                total * (1.0 / math.sqrt(HEAD)),
                jnp.zeros((plan.part, SIDE - HEAD), jnp.float32),
            ],
            axis=1,
        )
        return carry

    lax.fori_loop(0, plan.blocks, one_part, 0)


def first_head(plan, meta, queries, kv, later, within):
    nb = plan.blocks
    if plan.small:
        within_spec = pl.BlockSpec(within.shape, lambda i, m: (0, 0, 0))
    else:
        within_spec = pl.BlockSpec(memory_space=pl.ANY)
    return pl.pallas_call(
        functools.partial(first_kernel, plan),
        name="first_head",
        grid_spec=pltpu.PrefetchScalarGridSpec(
            num_scalar_prefetch=1,
            grid=(1,),
            in_specs=[
                pl.BlockSpec((nb, plan.part, SIDE), lambda i, m: (0, 0, 0)),
                pl.BlockSpec((plan.keys, SIDE), lambda i, m: (0, 0)),
                pl.BlockSpec((nb, plan.rows, SIDE), lambda i, m: (0, 0, 0)),
                within_spec,
            ],
            out_specs=[
                pl.BlockSpec((nb, plan.part, SIDE), lambda i, m: (0, 0, 0)),
                pl.BlockSpec((nb, plan.rows, SIDE), lambda i, m: (0, 0, 0)),
            ],
            scratch_shapes=[
                pltpu.VMEM((plan.part_pad, plan.rows), jnp.float32),
                pltpu.SemaphoreType.DMA,
            ],
        ),
        out_shape=[
            jax.ShapeDtypeStruct((nb, plan.part, SIDE), jnp.float32),
            jax.ShapeDtypeStruct((nb, plan.rows, SIDE), jnp.float32),
        ],
        compiler_params=pltpu.CompilerParams(vmem_limit_bytes=VMEM_LIMIT),
        cost_estimate=pl.CostEstimate(
            flops=6 * plan.rows * plan.keys * HEAD,
            bytes_accessed=1024 * plan.keys,
            transcendentals=0,
        ),
    )(meta, queries.reshape(nb, plan.part, plan.width), kv, later, within)


def body(
    tokens,
    lengths,
    deal_table,
    norm_one_gain,
    norm_one_bias,
    triple_weight,
    output_weight,
    norm_two_gain,
    norm_two_bias,
    up_weight,
    down_weight,
    cotangent,
):
    bf16, f32 = jnp.bfloat16, jnp.float32
    n_ctx = lax.axis_size("ctx")
    device = lax.axis_index("ctx")
    row_count, width = tokens.shape
    plan = Plan(row_count, n_ctx, lengths.shape[1], width)
    part_rows = plan.part
    head_scale = 1.0 / math.sqrt(HEAD)
    route_table = deal_table[0]
    counter = jnp.arange(n_ctx, dtype=jnp.int32)
    route_hits = route_table[:, :, None] == counter[None, None, :]
    inverse = jnp.sum(jnp.where(route_hits, counter[None, :, None], 0), axis=1)
    my_parts = jnp.take(inverse, device, axis=0)
    my_slots = jnp.take(inverse, device, axis=1)
    my_owners = jnp.take(route_table, device, axis=0)
    part_first = counter[:, None] * row_count + inverse * part_rows
    my_first = counter * row_count + my_slots * part_rows
    meta = jnp.concatenate([lengths[0], my_slots])

    gain_one, bias_one, triple_full, output_full, gain_two, bias_two, up_full, down_full = (
        lax.all_gather(norm_one_gain, "fsdp", axis=0, tiled=True),
        lax.all_gather(norm_one_bias, "fsdp", axis=0, tiled=True),
        lax.all_gather(triple_weight, "fsdp", axis=0, tiled=True),
        lax.all_gather(output_weight, "fsdp", axis=0, tiled=True),
        lax.all_gather(norm_two_gain, "fsdp", axis=0, tiled=True),
        lax.all_gather(norm_two_bias, "fsdp", axis=0, tiled=True),
        lax.all_gather(up_weight, "fsdp", axis=0, tiled=True),
        lax.all_gather(down_weight, "fsdp", axis=0, tiled=True),
    )
    gain_one = gain_one.astype(f32)
    bias_one = bias_one.astype(f32)
    gain_two = gain_two.astype(f32)
    bias_two = bias_two.astype(f32)

    outgoing = jnp.take(tokens.reshape(n_ctx, part_rows, width), my_parts, axis=0)
    dealt = lax.all_to_all(outgoing, "ctx", split_axis=0, concat_axis=0, tiled=True).reshape(
        row_count, width
    )
    natural = tokens.astype(f32)
    resid = dealt.astype(f32)
    hidden_nat = layer_norm(natural, gain_one, bias_one).astype(bf16)
    hidden_one = layer_norm(resid, gain_one, bias_one).astype(bf16)
    kv_part = matmul(hidden_nat, triple_full[:, width:]).astype(bf16)
    side_part = (matmul(hidden_nat, triple_full[:, :SIDE]).astype(bf16) * head_scale).astype(bf16)
    queries = (matmul(hidden_one, triple_full[:, :width]).astype(bf16) * head_scale).astype(bf16)
    kv = lax.all_gather(
        jnp.concatenate([kv_part, side_part], axis=1), "ctx", axis=0, tiled=True
    )

    high, low, total = attend(plan, meta, queries, kv)
    mixed_low = high.reshape(row_count, width)
    middle = resid + matmul(mixed_low, output_full)
    hidden_two = layer_norm(middle, gain_two, bias_two).astype(bf16)
    raised = matmul(hidden_two, up_full)
    activated = jax.nn.gelu(raised).astype(bf16)
    result = (middle + matmul(activated, down_full)).astype(bf16)
    grad_final = cotangent.astype(f32)
    grad_down = dot_tn(activated, cotangent).astype(bf16)
    grad_raised = gelu_back(raised, dot_nt(cotangent, down_full)).astype(bf16)
    grad_up = dot_tn(hidden_two, grad_raised).astype(bf16)
    grad_hidden_two = dot_nt(grad_raised, up_full)
    grad_mid_norm, grad_gain_two, grad_bias_two = norm_back(middle, gain_two, grad_hidden_two)
    grad_middle = grad_final + grad_mid_norm
    grad_attended = grad_middle.astype(bf16)
    grad_output = dot_tn(mixed_low, grad_attended).astype(bf16)
    grad_mixed = dot_nt(grad_attended, output_full)

    dq, dk, dv, within, sums = attend_back(
        plan, meta, queries, grad_mixed, high, low, total, kv
    )
    sums = sums.reshape(plan.keys, SIDE)[:, part_rows : part_rows + n_ctx]
    all_sums = lax.all_gather(sums.T, "ctx", axis=0, tiled=False)
    order = inverse.T * part_rows + counter[None, :] * row_count
    is_later = order.reshape(-1)[:, None] > my_first[None, :]
    is_later = jnp.pad(is_later.astype(f32), ((0, 0), (0, SIDE - n_ctx)))
    later = lax.dot_general(
        all_sums.reshape(n_ctx * n_ctx, plan.keys),
        is_later,
        (((0,), (0,)), ((), ())),
        precision=lax.Precision.HIGHEST,
        preferred_element_type=f32,
    ).reshape(n_ctx, row_count, SIDE)
    dq_extra, dk_extra = first_head(plan, meta, queries, kv, later, within)

    key_sum = lax.psum_scatter(
        dk.reshape(plan.keys, width), "ctx", scatter_dimension=0, tiled=True
    )
    value_sum = lax.psum_scatter(
        dv.reshape(plan.keys, width), "ctx", scatter_dimension=0, tiled=True
    )
    extra_sum = lax.psum_scatter(
        dk_extra.reshape(plan.keys, SIDE), "ctx", scatter_dimension=0, tiled=True
    )
    grad_q = dq.reshape(row_count, width) + jnp.pad(
        dq_extra.reshape(row_count, SIDE), ((0, 0), (0, width - SIDE))
    )
    grad_q = grad_q.astype(bf16)
    grad_key = key_sum.astype(f32) + jnp.pad(extra_sum, ((0, 0), (0, width - SIDE)))
    grad_kv = jnp.concatenate([grad_key.astype(bf16), value_sum], axis=1)

    back_q = dot_nt(grad_q, triple_full[:, :width])
    dealt_in, gain_a, bias_a = norm_back(resid, gain_one, back_q)
    grad_dealt = (grad_middle + dealt_in).astype(bf16)
    returned = lax.all_to_all(
        grad_dealt.reshape(n_ctx, part_rows, width), "ctx", split_axis=0, concat_axis=0, tiled=True
    )
    returned = jnp.take(returned, my_owners, axis=0).reshape(row_count, width)
    back_kv = dot_nt(grad_kv, triple_full[:, width:])
    natural_in, gain_b, bias_b = norm_back(natural, gain_one, back_kv)
    token_grad = returned.astype(f32) + natural_in
    grad_triple = jnp.concatenate(
        [dot_tn(hidden_one, grad_q), dot_tn(hidden_nat, grad_kv)], axis=1
    ).astype(bf16)

    shard_triple, shard_output, shard_up, shard_down = (
        lax.psum_scatter(grad_triple, "fsdp", scatter_dimension=0, tiled=True),
        lax.psum_scatter(grad_output, "fsdp", scatter_dimension=0, tiled=True),
        lax.psum_scatter(grad_up, "fsdp", scatter_dimension=0, tiled=True),
        lax.psum_scatter(grad_down, "fsdp", scatter_dimension=0, tiled=True),
    )
    sum_triple, sum_output, sum_up, sum_down = lax.psum(
        (shard_triple, shard_output, shard_up, shard_down), "ctx"
    )
    vectors = lax.psum(
        jnp.stack([gain_a + gain_b, bias_a + bias_b, grad_gain_two, grad_bias_two]),
        ("ctx", "fsdp"),
    )
    slot = width // lax.axis_size("fsdp")
    vectors = lax.dynamic_slice_in_dim(vectors, lax.axis_index("fsdp") * slot, slot, axis=1)
    return (
        result,
        token_grad,
        vectors[0],
        vectors[1],
        sum_triple.astype(f32),
        sum_output.astype(f32),
        vectors[2],
        vectors[3],
        sum_up.astype(f32),
        sum_down.astype(f32),
    )


def solution(mesh):
    rows = P(("ctx", "fsdp"), None)
    shard = P("fsdp")
    matrix = P("fsdp", None)
    return jax.shard_map(
        body,
        mesh=mesh,
        in_specs=(
            rows,
            matrix,
            P("fsdp", None, None),
            shard,
            shard,
            matrix,
            matrix,
            shard,
            shard,
            matrix,
            matrix,
            rows,
        ),
        out_specs=(rows, rows, shard, shard, matrix, matrix, shard, shard, matrix, matrix),
        check_vma=False,
    )
```
